32 devices in a mesh: section: 2 (over x), expert: 16 (over z, y, core).
Axes of the slice: x: 2, y: 2, z: 4, core: 2. Of those that a mesh axis runs over, the one named last changes fastest.
Arguments:
- grad_out: bfloat16 [2, 2048, 4096], P('section', 'expert'), may hold values from -6 to 6
- expert_ids: int32 [2, 2048, 8], P('section', 'expert'), may hold values from 0 to 15, all different within a row; in each aligned block of 128 rows (0 to 127, 128 to 255, ..., all dimensions but the last counted through in order) at most 72 rows name the same one
- gate_weights: float32 [2, 2048, 8], P('section', 'expert'), may hold values from 0.05 to 0.6
- saved_gate: bfloat16 [2, 16, 1152, 768], P('section', 'expert'), may hold values from -6 to 6
- saved_up: bfloat16 [2, 16, 1152, 768], P('section', 'expert'), may hold values from -6 to 6
- w_gate: bfloat16 [2, 16, 4096, 768], P('section', 'expert'), may hold values from -0.09375 to 0.09375
- w_up: bfloat16 [2, 16, 4096, 768], P('section', 'expert'), may hold values from -0.09375 to 0.09375
- w_down: bfloat16 [2, 16, 768, 4096], P('section', 'expert'), may hold values from -0.21875 to 0.21875
Outputs:
- upstream: bfloat16 [2, 2048, 4096], P('section', 'expert')
The draws below stay inside these ranges and needn't reach their ends.
Inputs may be any that keep to these rules, and one draw needn't show every extreme that they name: `expert_ids`: each token names 8 different experts of its section's 16; no expert is named by more than 72 of the tokens of one device, a bound that some block reaches of some device in every draw.
All inputs are finite; a program needn't handle non-finite values.
Results may differ from the reference program's by a relative error of at most 0.0057.
Values may be sent and summed in bfloat16 or wider, within the bound.
No kernel may reach another device: no remote copies, remote signals or barrier semaphores. Data moves between devices by JAX's collectives and lax.ppermute only.
A program may use at most 128 MiB of HBM per device.

```python
import math
import jax
import jax.numpy as jnp
import numpy as np
from jax import lax

D = 4096
H = 768
TOPK = 8
TOK_DEV = 128
SECTIONS = 2
EXPERTS = 16
TOKENS = 2048
MOST = 72
SLOTS = 1152


def block_scale(key, shape, pieces, smallest, largest):
    gain, own = 1.0, jax.random.fold_in(key, 6)
    for dim, parts in pieces:
        steps = jnp.exp(jax.random.uniform(jax.random.fold_in(own, dim), (parts,), jnp.float32, smallest / len(pieces), largest / len(pieces)))
        gain = gain * jnp.repeat(steps, shape[dim] // parts).reshape([-1 if axis == dim else 1 for axis in range(len(shape))])
    return gain


def deal_out(stream_key, own, number, rows, number_of, top, most, slope):
    order = jax.random.permutation(stream_key, number_of)
    packed, ordinary = load_shares(number_of, rows * top, most, slope, True), load_shares(number_of, rows * top, most, slope, False)
    places = jnp.arange(number_of)

    def named(lengths, offset_by):
        used = int((lengths > 0).sum())
        fixed = max(1, used // 4)
        moved = fixed + (places - fixed + offset_by * (used - fixed)) % max(1, number_of - fixed)
        return jnp.zeros((number_of,), jnp.int32).at[order[jnp.where(places < fixed, places, moved)]].set(jnp.asarray(lengths, jnp.int32))

    lengths = jnp.where(number % 4 == 0, named(packed, number // 4), named(ordinary, number - number // 4 - 1))
    mixed = jax.random.permutation(jax.random.fold_in(own, 3), number_of)
    source_of, receiver = mixed[0:number_of // 2 * 2:2], mixed[1:number_of // 2 * 2:2]
    margin = jnp.minimum(lengths[source_of] - 1, most - lengths[receiver]) // 2
    margin = jnp.where((source_of == order[0]) | (receiver == order[0]) | (lengths[receiver] == 0), 0, jnp.maximum(margin, 0))
    moved = jax.random.randint(jax.random.fold_in(own, 4), (number_of // 2,), 0, 1 << 20) % (margin + 1)
    lengths = lengths.at[source_of].add(-moved).at[receiver].add(moved)
    members = jnp.searchsorted(jnp.cumsum(lengths), jnp.arange(rows * top), side="right").astype(jnp.int32)
    grid = members.reshape(top, rows).T
    grid = grid[jax.random.permutation(jax.random.fold_in(own, 1), rows)]
    offset_by = jax.random.randint(jax.random.fold_in(own, 2), (rows, 1), 0, top)
    return jnp.take_along_axis(grid, (jnp.arange(top)[None, :] + offset_by) % top, axis=1)


def load_shares(amount, total, reach, lean, full):
    weights = [(1 << 20) // math.isqrt(rank ** lean) + 1 for rank in range(1, amount + 1)]
    largest = reach if full else min(reach, max(-(-total // amount), total * weights[0] // sum(weights)))
    least = 1 if total - largest >= amount - 1 else 0
    holding, surplus = [largest] + [least] * (amount - 1), total - largest - least * (amount - 1)
    while surplus > 0:
        movable = [i for i in range(1, amount) if holding[i] < largest] or [i for i in range(1, amount) if holding[i] < reach]
        whole, remaining = sum([weights[i] for i in movable]), surplus
        for i in movable:
            more = min(reach - holding[i], max(1, remaining * weights[i] // whole), surplus)
            holding[i] = holding[i] + more
            surplus = surplus - more
    return np.array(holding)


def noise(key, shape, scale, bound, pieces=(), held_as=jnp.bfloat16):
    drawn = scale * jax.random.normal(key, shape, jnp.float32)
    if pieces:
        drawn = drawn * block_scale(key, shape, pieces, -0.22, 0.18)
    return jnp.clip(drawn, -bound, bound).astype(held_as)


def setup_inputs(seed: int = 0) -> dict:
    arg_keys = jax.random.split(jax.random.key(seed), 9)
    grad_out = noise(arg_keys[0], (SECTIONS, TOKENS, D), 1.0, 6.0, ((0, 2), (1, 16)))
    expert_ids_keys = jax.random.split(jax.random.fold_in(arg_keys[1], 1), SECTIONS * TOKENS // TOK_DEV)
    expert_ids_turns = jax.random.permutation(jax.random.fold_in(arg_keys[1], 3), SECTIONS * TOKENS // TOK_DEV)
    expert_ids = jax.vmap(lambda own, number: deal_out(jax.random.fold_in(arg_keys[1], 2), own, number, TOK_DEV, EXPERTS, TOPK, MOST, 2))(expert_ids_keys, expert_ids_turns).reshape((SECTIONS, TOKENS, TOPK))
    gate_weights = jnp.clip(0.05 + 0.55 * jax.random.uniform(arg_keys[2], (SECTIONS, TOKENS, TOPK), jnp.float32) ** block_scale(arg_keys[2], (SECTIONS, TOKENS, TOPK), ((0, 2), (1, 16)), -0.2, 0.2), 0.05, 0.6)
    saved_gate = noise(arg_keys[3], (SECTIONS, EXPERTS, SLOTS, H), 1.5, 6.0, ((0, 2), (1, 16)))
    saved_up = noise(arg_keys[4], (SECTIONS, EXPERTS, SLOTS, H), 1.0, 6.0, ((0, 2), (1, 16)))
    w_gate = noise(arg_keys[5], (SECTIONS, EXPERTS, D, H), D ** -0.5, 0.09375, ((0, 2), (1, 16)))
    w_up = noise(arg_keys[6], (SECTIONS, EXPERTS, D, H), D ** -0.5, 0.09375, ((0, 2), (1, 16)))
    w_down = noise(arg_keys[7], (SECTIONS, EXPERTS, H, D), H ** -0.5, 0.21875, ((0, 2), (1, 16)))
    return {"grad_out": grad_out, "expert_ids": expert_ids, "gate_weights": gate_weights, "saved_gate": saved_gate, "saved_up": saved_up, "w_gate": w_gate, "w_up": w_up, "w_down": w_down}


def expert_backward(routed, pre_gate, pre_up, gate_matrix, up_matrix, down_matrix):
    contract = (((1,), (1,)), ((), ()))
    hidden_grad = lax.dot_general(routed, down_matrix, contract, preferred_element_type=jnp.float32)
    gate_value = pre_gate.astype(jnp.float32)
    up_value = pre_up.astype(jnp.float32)
    sigmoid_gate = jax.nn.sigmoid(gate_value)
    gate_grad = (hidden_grad * up_value * sigmoid_gate * (1.0 + gate_value * (1.0 - sigmoid_gate))).astype(jnp.bfloat16)
    up_grad = (hidden_grad * gate_value * sigmoid_gate).astype(jnp.bfloat16)
    result = lax.dot_general(gate_grad, gate_matrix, contract, preferred_element_type=jnp.float32)
    result = result + lax.dot_general(up_grad, up_matrix, contract, preferred_element_type=jnp.float32)
    return result.astype(jnp.bfloat16)


def slot_numbers(routing):
    experts = jnp.arange(EXPERTS, dtype=jnp.int32)
    onehot = jnp.sum((routing[:, :, None] == experts).astype(jnp.int32), axis=1)
    blocks = onehot.reshape(-1, TOK_DEV, EXPERTS)
    before = (jnp.cumsum(blocks, axis=1) - blocks).reshape(-1, EXPERTS).astype(jnp.int32)
    position = jnp.take_along_axis(before, routing, axis=1)
    device = (jnp.arange(routing.shape[0], dtype=jnp.int32) // TOK_DEV)[:, None]
    return (device * MOST + position).astype(jnp.int32)


def section_backward(grad_rows, routing, weights, saved_gate, saved_up, w_gate, w_up, w_down):
    slot_table = slot_numbers(routing)

    def one_expert(running, inputs):
        expert_number, pre_gate, pre_up, gate_matrix, up_matrix, down_matrix = inputs
        chosen = routing == expert_number
        is_routed = jnp.any(chosen, axis=1)
        slot_index = jnp.sum(jnp.where(chosen, slot_table, 0), axis=1).astype(jnp.int32)
        weight = jnp.sum(jnp.where(chosen, weights, jnp.zeros_like(weights)), axis=1)
        target = jnp.where(is_routed, slot_index, SLOTS).astype(jnp.int32)
        routed = jnp.zeros((SLOTS + 1, D), jnp.bfloat16).at[target].set(grad_rows)[:SLOTS]
        result = expert_backward(routed, pre_gate, pre_up, gate_matrix, up_matrix, down_matrix)
        picked = result[slot_index].astype(jnp.float32)
        return running + weight[:, None] * picked, None

    start = jnp.zeros((grad_rows.shape[0], D), jnp.float32)
    inputs = (jnp.arange(EXPERTS, dtype=jnp.int32), saved_gate, saved_up, w_gate, w_up, w_down)
    summed, unused = lax.scan(one_expert, start, inputs)
    return summed.astype(jnp.bfloat16)


def reference(grad_out, expert_ids, gate_weights, saved_gate, saved_up, w_gate, w_up, w_down):
    results = []
    for section_number in range(SECTIONS):
        results.append(section_backward(grad_out[section_number], expert_ids[section_number], gate_weights[section_number],
                                      saved_gate[section_number], saved_up[section_number], w_gate[section_number],
                                      w_up[section_number], w_down[section_number]))
    shifted = results[1:] + [jnp.zeros_like(results[0])]
    return jnp.stack(shifted, axis=0)
```

```python
import math

import jax
import jax.numpy as jnp
from jax import lax
from jax.sharding import PartitionSpec as P

PIECES = 2


def chip_ring(chips):
    width = 1 << (int(math.log2(chips)) // 2)
    height = chips // width
    tour = []
    for row in range(height):
        columns = list(range(1, width))
        if row % 2:
            columns.reverse()
        tour += [row * width + column for column in columns]
    return tour + [row * width for row in reversed(range(height))]


def body(grad_out, expert_ids, gate_weights, saved_gate, saved_up, w_gate, w_up, w_down):
    devices = lax.axis_size("expert")
    sections = lax.axis_size("section")
    chips = devices // 2
    tour = chip_ring(chips)
    following = {chip: tour[(k + 1) % chips] for k, chip in enumerate(tour)}
    onward = [(2 * a, 2 * b) for a, b in following.items()] + [(2 * b + 1, 2 * a + 1) for a, b in following.items()]
    swap = [(i, i ^ 1) for i in range(devices)]
    relay = [(s * devices + i, (s - 1) * devices + i) for s in range(1, sections) for i in range(devices)]
    relay_onward = [(s * devices + a, (s - 1) * devices + b) for s in range(1, sections) for a, b in onward]

    me = lax.axis_index("expert")
    core = me % 2
    tour_table = jnp.array(tour, jnp.int32)
    place = jnp.argmax(tour_table == me // 2).astype(jnp.int32)

    def source(step, side):
        place_there = jnp.where(side == 0, place - step, place + step) % chips
        return tour_table[place_there] * 2 + side

    rows = grad_out[0]
    tokens = rows.shape[0]
    hidden = saved_gate.shape[3]
    capacity = saved_gate.shape[2] // devices
    routing = expert_ids[0]
    experts = jnp.arange(devices, dtype=jnp.int32)
    chosen = routing[:, None, :] == experts[None, :, None]
    named = jnp.any(chosen, axis=2)
    weight_of = jnp.sum(jnp.where(chosen, gate_weights[0][:, None, :], 0.0), axis=2)
    earlier = jnp.tril(jnp.ones((tokens, tokens), jnp.bfloat16), -1)
    position = lax.dot_general(
        earlier, named.astype(jnp.bfloat16), (((1,), (0,)), ((), ())), preferred_element_type=jnp.float32
    )
    position = jnp.where(named, position, -1.0)
    table = jnp.stack([position.T, weight_of.T], axis=1)
    table = lax.all_to_all(table, "expert", split_axis=0, concat_axis=0, tiled=True)

    piece = tokens // PIECES
    blocks = [[rows[h * piece:(h + 1) * piece] for h in range(PIECES)]]
    for step in range(1, chips):
        blocks.append([lax.ppermute(b, "expert", onward) for b in blocks[-1]])
    others = [[lax.ppermute(b, "expert", swap) for b in held] for held in blocks]

    gate_rows = saved_gate[0, 0].reshape(devices, capacity, hidden)
    up_rows = saved_up[0, 0].reshape(devices, capacity, hidden)
    contract = (((1,), (1,)), ((), ()))

    def expert_step(step):
        here, there = source(step, core), source(step, 1 - core)
        block = jnp.concatenate(blocks[step] + others[step], axis=0)
        gates, ups, scales = [], [], []
        for origin in (here, there):
            entry = lax.dynamic_index_in_dim(table, origin, 0, keepdims=False)
            pick = (entry[0][:, None] == jnp.arange(capacity, dtype=jnp.float32)).astype(jnp.bfloat16)
            for out, saved in ((gates, gate_rows), (ups, up_rows)):
                out.append(pick @ lax.dynamic_index_in_dim(saved, origin, 0, keepdims=False))
            scales.append(entry[1])
        gate = jnp.concatenate(gates, axis=0).astype(jnp.float32)
        up = jnp.concatenate(ups, axis=0).astype(jnp.float32)
        scale = jnp.concatenate(scales, axis=0)
        hidden_grad = lax.dot_general(block, w_down[0, 0], contract, preferred_element_type=jnp.float32)
        sig = jax.nn.sigmoid(gate)
        gate_grad = (hidden_grad * up * sig * (1.0 + gate * (1.0 - sig))).astype(jnp.bfloat16)
        up_grad = (hidden_grad * gate * sig).astype(jnp.bfloat16)
        back = lax.dot_general(gate_grad, w_gate[0, 0], contract, preferred_element_type=jnp.float32)
        back = back + lax.dot_general(up_grad, w_up[0, 0], contract, preferred_element_type=jnp.float32)
        partial = (back * scale[:, None]).astype(jnp.bfloat16)
        return [partial[h * piece:(h + 1) * piece] for h in range(2 * PIECES)]

    def chip_sum(step):
        parts = expert_step(step)
        given = [lax.ppermute(p, "expert", swap) for p in parts[PIECES:]]
        return [a.astype(jnp.float32) + b.astype(jnp.float32) for a, b in zip(parts[:PIECES], given)]

    own = [c.astype(jnp.bfloat16) for c in chip_sum(0)]
    own = [lax.ppermute(c, ("section", "expert"), relay) for c in own]
    running = [c.astype(jnp.bfloat16) for c in chip_sum(1)]
    for step in range(2, chips):
        arrived = [lax.ppermute(r, "expert", onward) for r in running]
        running = [
            (a.astype(jnp.float32) + c).astype(jnp.bfloat16) for a, c in zip(arrived, chip_sum(step))
        ]
    last = [lax.ppermute(r, ("section", "expert"), relay_onward) for r in running]
    result = [(a.astype(jnp.float32) + b.astype(jnp.float32)).astype(jnp.bfloat16) for a, b in zip(last, own)]
    return jnp.concatenate(result, axis=0)[None]


def solution(mesh):
    placed = (
        P("section", "expert", None),
        P("section", "expert", None),
        P("section", "expert", None),
        P("section", "expert", None, None),
        P("section", "expert", None, None),
        P("section", "expert", None, None),
        P("section", "expert", None, None),
        P("section", "expert", None, None),
    )
    return jax.shard_map(
        body, mesh=mesh, in_specs=placed, out_specs=P("section", "expert", None), check_vma=False
    )
```

```python
import functools
import math

import jax
import jax.numpy as jnp
import numpy as np
from jax import lax
from jax.experimental import pallas as pl
from jax.experimental.pallas import tpu as pltpu
from jax.sharding import PartitionSpec as P

PIECES = 2
CONTRACT = (((1,), (1,)), ((), ()))


def chip_ring(chips):
    width = 1 << (int(math.log2(chips)) // 2)
    height = chips // width
    tour = []
    for row in range(height):
        columns = list(range(1, width))
        if row % 2:
            columns.reverse()
        tour += [row * width + column for column in columns]
    return tour + [row * width for row in reversed(range(height))]


def origin_table(devices, tour):
    chips = len(tour)
    place = {chip: k for k, chip in enumerate(tour)}
    table = np.zeros((devices, chips, 2), np.int32)
    for device in range(devices):
        at = place[device // 2]
        for step in range(chips):
            by_core = [2 * tour[(at - step) % chips], 2 * tour[(at + step) % chips] + 1]
            table[device, step] = by_core[device % 2], by_core[1 - device % 2]
    return table


def expert_kernel(
    origin, a0, a1, b0, b1, table, saved_gate, saved_up, w_down, w_gate, w_up, mine0, mine1, given0, given1,
    block, entry, gate_rows, up_rows, down_v, gate_v, up_v, gate_grad, up_grad, scale, out_mine, out_given,
    block_sem, entry_sem, rows_sem, down_sem, wide_sem, out_sem,
):
    piece, width = a0.shape
    tokens = 2 * piece
    hidden_parts, hidden_block = down_v.shape[0], down_v.shape[1]
    parts, part = gate_v.shape[0], gate_v.shape[1]
    capacity = gate_rows.shape[1]

    def block_copy(n):
        return pltpu.make_async_copy((a0, a1, b0, b1)[n], block.at[pl.ds(n * piece, piece)], block_sem.at[n])

    def entry_copy(n):
        return pltpu.make_async_copy(table.at[origin[n]], entry.at[n], entry_sem.at[n])

    def gate_rows_copy(n):
        return pltpu.make_async_copy(saved_gate.at[origin[n]], gate_rows.at[n], rows_sem.at[n])

    def up_rows_copy(n):
        return pltpu.make_async_copy(saved_up.at[origin[n]], up_rows.at[n], rows_sem.at[2 + n])

    def down_copy(n):
        return pltpu.make_async_copy(w_down.at[pl.ds(n * hidden_block, hidden_block)], down_v.at[n], down_sem.at[n])

    def gate_copy(n):
        return pltpu.make_async_copy(w_gate.at[pl.ds(n * part, part)], gate_v.at[n], wide_sem.at[n])

    def up_copy(n):
        return pltpu.make_async_copy(w_up.at[pl.ds(n * part, part)], up_v.at[n], wide_sem.at[parts + n])

    for n in range(4):
        block_copy(n).start()
    down_copy(0).start()
    for n in range(2):
        entry_copy(n).start()
        gate_rows_copy(n).start()
        up_rows_copy(n).start()
    for n in range(1, hidden_parts):
        down_copy(n).start()
    for n in range(2):
        entry_copy(n).wait()
        gate_rows_copy(n).wait()
        up_rows_copy(n).wait()
    picks = []
    for n in range(2):
        place = jnp.broadcast_to(entry[n, 0:1, :], (tokens, tokens)).T
        slot = lax.broadcasted_iota(jnp.int32, (tokens, tokens), 1).astype(jnp.float32)
        picks.append(jnp.where(place == slot, 1.0, 0.0).astype(jnp.bfloat16)[:, :capacity])
        scale[pl.ds(n * tokens, tokens), :] = jnp.broadcast_to(entry[n, 1:2, :], (tokens, tokens)).T
    for n in range(4):
        block_copy(n).wait()

    for k in range(hidden_parts):
        columns = pl.ds(k * hidden_block, hidden_block)
        down_copy(k).wait()
        for n in range(parts * k // hidden_parts, parts * (k + 1) // hidden_parts):
            gate_copy(n).start()
            up_copy(n).start()
        hidden_grad = lax.dot_general(block[...], down_v[k], CONTRACT, preferred_element_type=jnp.float32)
        for n in range(2):
            gate = jnp.dot(picks[n], gate_rows[n, :, columns], preferred_element_type=jnp.float32)
            up = jnp.dot(picks[n], up_rows[n, :, columns], preferred_element_type=jnp.float32)
            sig = 1.0 / (1.0 + jnp.exp(-gate))
            grad = hidden_grad[n * tokens:(n + 1) * tokens] * sig
            rows = pl.ds(n * tokens, tokens)
            gate_grad[rows, columns] = (grad * up * (1.0 + gate * (1.0 - sig))).astype(jnp.bfloat16)
            up_grad[rows, columns] = (grad * gate).astype(jnp.bfloat16)

    outs = (mine0, mine1, given0, given1)

    def out_copy(j, n):
        held = (out_mine, out_mine, out_given, out_given)[n]
        return pltpu.make_async_copy(
            held.at[j, pl.ds((n % 2) * piece, piece)],
            outs[n].at[:, pl.ds(pl.multiple_of(j * part, part), part)],
            out_sem.at[j, n],
        )

    def wide_step(j, carry):
        gate_copy(j).wait()
        up_copy(j).wait()
        back = lax.dot_general(gate_grad[...], gate_v[j], CONTRACT, preferred_element_type=jnp.float32)
        back = back + lax.dot_general(up_grad[...], up_v[j], CONTRACT, preferred_element_type=jnp.float32)
        back = back.astype(jnp.bfloat16).astype(jnp.float32) * scale[:, 0:1]
        out_mine[j] = back[:tokens]
        out_given[j] = back[tokens:].astype(jnp.bfloat16)
        for n in range(4):
            out_copy(j, n).start()
        return carry

    lax.fori_loop(0, parts, wide_step, 0)

    def drain(j, carry):
        for n in range(4):
            out_copy(j, n).wait()
        return carry

    lax.fori_loop(0, parts, drain, 0)


def expert_step(origin, held, other, table, gate_rows, up_rows, w_down, w_gate, w_up):
    piece, width = held[0].shape
    tokens = 2 * piece
    hidden = w_down.shape[0]
    capacity = gate_rows.shape[1]
    hidden_block, part = 256, 512
    hidden_parts, parts = hidden // hidden_block, width // part
    anywhere = pl.BlockSpec(memory_space=pl.ANY)
    bf16, f32 = jnp.bfloat16, jnp.float32
    dma = pltpu.SemaphoreType.DMA
    flops = 2 * 2 * tokens * hidden * width * 3
    moved = 2 * 3 * hidden * width + 2 * tokens * width * 5
    return pl.pallas_call(
        expert_kernel,
        in_specs=[pl.BlockSpec(memory_space=pltpu.SMEM)] + [anywhere] * 10,
        out_specs=[anywhere] * 4,
        out_shape=[jax.ShapeDtypeStruct((piece, width), f32)] * 2 + [jax.ShapeDtypeStruct((piece, width), bf16)] * 2,
        scratch_shapes=[
            pltpu.VMEM((2 * tokens, width), bf16),
            pltpu.VMEM((2,) + table.shape[1:], f32),
            pltpu.VMEM((2, capacity, hidden), bf16),
            pltpu.VMEM((2, capacity, hidden), bf16),
            pltpu.VMEM((hidden_parts, hidden_block, width), bf16),
            pltpu.VMEM((parts, part, hidden), bf16),
            pltpu.VMEM((parts, part, hidden), bf16),
            pltpu.VMEM((2 * tokens, hidden), bf16),
            pltpu.VMEM((2 * tokens, hidden), bf16),
            pltpu.VMEM((2 * tokens, tokens), f32),
            pltpu.VMEM((parts, tokens, part), f32),
            pltpu.VMEM((parts, tokens, part), bf16),
            dma((4,)),
            dma((2,)),
            dma((4,)),
            dma((hidden_parts,)),
            dma((2 * parts,)),
            dma((parts, 4)),
        ],
        compiler_params=pltpu.CompilerParams(vmem_limit_bytes=40 << 20),
        cost_estimate=pl.CostEstimate(flops=flops, transcendentals=2 * tokens * hidden, bytes_accessed=moved),
        name="expert_step",
    )(origin, *held, *other, table, gate_rows, up_rows, w_down, w_gate, w_up)


def body(grad_out, expert_ids, gate_weights, saved_gate, saved_up, w_gate, w_up, w_down):
    devices = lax.axis_size("expert")
    sections = lax.axis_size("section")
    chips = devices // 2
    tour = chip_ring(chips)
    following = {chip: tour[(k + 1) % chips] for k, chip in enumerate(tour)}
    onward = [(2 * a, 2 * b) for a, b in following.items()] + [(2 * b + 1, 2 * a + 1) for a, b in following.items()]
    swap = [(i, i ^ 1) for i in range(devices)]
    relay = [(s * devices + i, (s - 1) * devices + i) for s in range(1, sections) for i in range(devices)]
    relay_onward = [(s * devices + a, (s - 1) * devices + b) for s in range(1, sections) for a, b in onward]

    me = lax.axis_index("expert")
    origins = lax.dynamic_index_in_dim(jnp.asarray(origin_table(devices, tour)), me, 0, keepdims=False)

    rows = grad_out[0]
    tokens = rows.shape[0]
    hidden = saved_gate.shape[3]
    capacity = saved_gate.shape[2] // devices
    piece = tokens // PIECES
    first = [rows[h * piece:(h + 1) * piece] for h in range(PIECES)]
    first, routing, weights = lax.optimization_barrier((first, expert_ids[0], gate_weights[0]))

    blocks = [first]
    for step in range(1, chips):
        with jax.named_scope(f"gather_{step}"):
            blocks.append([lax.ppermute(b, "expert", onward) for b in blocks[-1]])
    others = []
    for step in range(chips):
        with jax.named_scope(f"share_{step}"):
            others.append([lax.ppermute(b, "expert", swap) for b in blocks[step]])

    with jax.named_scope("routing"):
        experts = jnp.arange(devices, dtype=jnp.int32)
        chosen = routing[:, None, :] == experts[None, :, None]
        named = jnp.any(chosen, axis=2)
        weight_of = jnp.sum(jnp.where(chosen, weights[:, None, :], 0.0), axis=2)
        earlier = jnp.tril(jnp.ones((tokens, tokens), jnp.bfloat16), -1)
        position = lax.dot_general(
            earlier, named.astype(jnp.bfloat16), (((1,), (0,)), ((), ())), preferred_element_type=jnp.float32
        )
        position = jnp.where(named, position, -1.0)
        table = jnp.stack([position.T, weight_of.T], axis=1)
        table = lax.all_to_all(table, "expert", split_axis=0, concat_axis=0, tiled=True)

    gate_rows = saved_gate[0, 0].reshape(devices, capacity, hidden)
    up_rows = saved_up[0, 0].reshape(devices, capacity, hidden)

    running = own = None
    token = origins
    for step in range(chips):
        with jax.named_scope(f"expert_{step}"):
            parts = expert_step(
                token[step], blocks[step], others[step], table, gate_rows, up_rows, w_down[0, 0], w_gate[0, 0], w_up[0, 0]
            )
            token, *parts = lax.optimization_barrier((token, *parts))
        with jax.named_scope(f"give_{step}"):
            given = [lax.ppermute(p, "expert", swap) for p in parts[PIECES:]]
        total = [a + b.astype(jnp.float32) for a, b in zip(parts[:PIECES], given)]
        if step == 0:
            with jax.named_scope("relay_own"):
                own = [lax.ppermute(c.astype(jnp.bfloat16), ("section", "expert"), relay) for c in total]
        elif step == 1:
            running = [c.astype(jnp.bfloat16) for c in total]
        else:
            with jax.named_scope(f"reduce_{step}"):
                arrived = [lax.ppermute(r, "expert", onward) for r in running]
                running = [(a.astype(jnp.float32) + c).astype(jnp.bfloat16) for a, c in zip(arrived, total)]
    with jax.named_scope("relay_last"):
        last = [lax.ppermute(r, ("section", "expert"), relay_onward) for r in running]
    result = [(a.astype(jnp.float32) + b.astype(jnp.float32)).astype(jnp.bfloat16) for a, b in zip(last, own)]
    return jnp.concatenate(result, axis=0)[None]


def solution(mesh):
    placed = (
        P("section", "expert", None),
        P("section", "expert", None),
        P("section", "expert", None),
        P("section", "expert", None, None),
        P("section", "expert", None, None),
        P("section", "expert", None, None),
        P("section", "expert", None, None),
        P("section", "expert", None, None),
    )
    return jax.shard_map(
        body, mesh=mesh, in_specs=placed, out_specs=P("section", "expert", None), check_vma=False
    )
```

```python
import math

import jax
import jax.numpy as jnp
import numpy as np
from jax import lax
from jax.experimental import pallas as pl
from jax.experimental.pallas import tpu as pltpu
from jax.sharding import PartitionSpec as P


PIECES = 2
HIDDEN_BLOCK = 256
PART = 512
VMEM_LIMIT = 16 << 20
CONTRACT = (((1,), (1,)), ((), ()))


def chip_ring(chips):
    width = 1 << (int(math.log2(chips)) // 2)
    height = chips // width
    tour = []
    for row in range(height):
        columns = list(range(1, width))
        if row % 2:
            columns.reverse()
        tour += [row * width + column for column in columns]
    return tour + [row * width for row in reversed(range(height))]


def origin_table(devices, tour):
    chips = len(tour)
    place = {chip: k for k, chip in enumerate(tour)}
    table = np.zeros((devices, chips, 2), np.int32)
    for device in range(devices):
        at = place[device // 2]
        for step in range(chips):
            by_core = [2 * tour[(at - step) % chips], 2 * tour[(at + step) % chips] + 1]
            table[device, step] = by_core[device % 2], by_core[1 - device % 2]
    return table


def expert_kernel(
    origin, a0, a1, b0, b1, table, saved_gate, saved_up, w_down, w_gate, w_up, mine0, mine1, given0, given1,
    block, entry, gate_rows, up_rows, gate_slope, up_slope, gate_grad, up_grad, scale, out_mine, out_given,
    block_sem, entry_sem, rows_sem, out_sem,
):
    piece, _ = a0.shape
    tokens = 2 * piece
    hidden = w_down.shape[0]
    parts, _, part = out_mine.shape
    capacity = gate_rows.shape[1]

    def block_copy(n):
        return pltpu.make_async_copy((a0, a1, b0, b1)[n], block.at[pl.ds(n * piece, piece)], block_sem.at[n])

    def entry_copy(n):
        return pltpu.make_async_copy(table.at[origin[n]], entry.at[n], entry_sem.at[n])

    def gate_rows_copy(n):
        return pltpu.make_async_copy(saved_gate.at[origin[n]], gate_rows.at[n], rows_sem.at[n])

    def up_rows_copy(n):
        return pltpu.make_async_copy(saved_up.at[origin[n]], up_rows.at[n], rows_sem.at[2 + n])

    for n in range(2):
        entry_copy(n).start()
        gate_rows_copy(n).start()
        up_rows_copy(n).start()
    for n in range(4):
        block_copy(n).start()
    for n in range(2):
        entry_copy(n).wait()
        gate_rows_copy(n).wait()
        up_rows_copy(n).wait()
    for n in range(2):
        rows = pl.ds(n * tokens, tokens)
        place = jnp.broadcast_to(entry[n, 0:1, :], (tokens, tokens)).T
        slot = lax.broadcasted_iota(jnp.int32, (tokens, tokens), 1).astype(jnp.float32)
        pick = jnp.where(place == slot, 1.0, 0.0).astype(jnp.bfloat16)[:, :capacity]
        scale[rows, :] = jnp.broadcast_to(entry[n, 1:2, :], (tokens, tokens)).T
        gate = jnp.dot(pick, gate_rows[n], preferred_element_type=jnp.float32)
        up = jnp.dot(pick, up_rows[n], preferred_element_type=jnp.float32)
        sig = 1.0 / (1.0 + jnp.exp(-gate))
        gate_slope[rows, :] = up * sig * (1.0 + gate * (1.0 - sig))
        up_slope[rows, :] = gate * sig
    for n in range(4):
        block_copy(n).wait()

    for k in range(hidden // HIDDEN_BLOCK):
        columns = pl.ds(k * HIDDEN_BLOCK, HIDDEN_BLOCK)
        hidden_grad = lax.dot_general(block[...], w_down[columns, :], CONTRACT, preferred_element_type=jnp.float32)
        gate_grad[:, columns] = (hidden_grad * gate_slope[:, columns]).astype(jnp.bfloat16)
        up_grad[:, columns] = (hidden_grad * up_slope[:, columns]).astype(jnp.bfloat16)

    outs = (mine0, mine1, given0, given1)

    def out_copy(j, n):
        held = (out_mine, out_mine, out_given, out_given)[n]
        return pltpu.make_async_copy(
            held.at[j, pl.ds((n % 2) * piece, piece)],
            outs[n].at[:, pl.ds(pl.multiple_of(j * part, part), part)],
            out_sem.at[j, n],
        )

    def wide_step(j, carry):
        columns = pl.ds(pl.multiple_of(j * part, part), part)
        back = lax.dot_general(gate_grad[...], w_gate[columns, :], CONTRACT, preferred_element_type=jnp.float32)
        back = back + lax.dot_general(up_grad[...], w_up[columns, :], CONTRACT, preferred_element_type=jnp.float32)
        back = back.astype(jnp.bfloat16).astype(jnp.float32) * scale[:, 0:1]
        out_mine[j] = back[:tokens]
        out_given[j] = back[tokens:].astype(jnp.bfloat16)
        for n in range(4):
            out_copy(j, n).start()
        return carry

    lax.fori_loop(0, parts, wide_step, 0)

    def drain(j, carry):
        for n in range(4):
            out_copy(j, n).wait()
        return carry

    lax.fori_loop(0, parts, drain, 0)


def expert_step(origin, held, other, table, gate_rows, up_rows, w_down, w_gate, w_up):
    piece, width = held[0].shape
    tokens = 2 * piece
    hidden = w_down.shape[0]
    capacity = gate_rows.shape[1]
    parts = width // PART
    anywhere, inside = pl.BlockSpec(memory_space=pl.ANY), pl.BlockSpec(memory_space=pltpu.VMEM)
    bf16, f32 = jnp.bfloat16, jnp.float32
    dma = pltpu.SemaphoreType.DMA
    flops = 2 * 2 * tokens * hidden * width * 3
    moved = 2 * tokens * width * 10
    weights = [pltpu.with_memory_space_constraint(w, pltpu.VMEM) for w in (w_down, w_gate, w_up)]
    return pl.pallas_call(
        expert_kernel,
        in_specs=[pl.BlockSpec(memory_space=pltpu.SMEM)] + [anywhere] * 7 + [inside] * 3,
        out_specs=[anywhere] * 4,
        out_shape=[jax.ShapeDtypeStruct((piece, width), f32)] * 2 + [jax.ShapeDtypeStruct((piece, width), bf16)] * 2,
        scratch_shapes=[
            pltpu.VMEM((2 * tokens, width), bf16),
            pltpu.VMEM((2,) + table.shape[1:], f32),
            pltpu.VMEM((2, capacity, hidden), bf16),
            pltpu.VMEM((2, capacity, hidden), bf16),
            pltpu.VMEM((2 * tokens, hidden), f32),
            pltpu.VMEM((2 * tokens, hidden), f32),
            pltpu.VMEM((2 * tokens, hidden), bf16),
            pltpu.VMEM((2 * tokens, hidden), bf16),
            pltpu.VMEM((2 * tokens, tokens), f32),
            pltpu.VMEM((parts, tokens, PART), f32),
            pltpu.VMEM((parts, tokens, PART), bf16),
            dma((4,)),
            dma((2,)),
            dma((4,)),
            dma((parts, 4)),
        ],
        compiler_params=pltpu.CompilerParams(vmem_limit_bytes=VMEM_LIMIT),
        cost_estimate=pl.CostEstimate(flops=flops, transcendentals=2 * tokens * hidden, bytes_accessed=moved),
        name="expert_step",
    )(origin, *held, *other, table, gate_rows, up_rows, *weights)


def load_kernel(*refs):
    count = len(refs) // 2
    sources, targets, sem = refs[:count], refs[count:2 * count], refs[2 * count]
    copies = [pltpu.make_async_copy(sources[n], targets[n], sem.at[n]) for n in range(count)]
    for copy in copies:
        copy.start()
    for copy in copies:
        copy.wait()


def load_inside(*arrays):
    return pl.pallas_call(
        load_kernel,
        in_specs=[pl.BlockSpec(memory_space=pltpu.HBM)] * len(arrays),
        out_specs=[pl.BlockSpec(memory_space=pltpu.VMEM)] * len(arrays),
        out_shape=[pltpu.VMEM(a.shape, a.dtype) for a in arrays],
        scratch_shapes=[pltpu.SemaphoreType.DMA((len(arrays),))],
        compiler_params=pltpu.CompilerParams(vmem_limit_bytes=VMEM_LIMIT),
        name="load_weights",
    )(*[pltpu.with_memory_space_constraint(a, pltpu.HBM) for a in arrays])


def body(grad_out, expert_ids, gate_weights, saved_gate, saved_up, w_gate, w_up, w_down):
    devices = lax.axis_size("expert")
    sections = lax.axis_size("section")
    chips = devices // 2
    tour = chip_ring(chips)
    following = {chip: tour[(k + 1) % chips] for k, chip in enumerate(tour)}
    onward = [(2 * a, 2 * b) for a, b in following.items()] + [(2 * b + 1, 2 * a + 1) for a, b in following.items()]
    swap = [(i, i ^ 1) for i in range(devices)]
    relay = [(s * devices + i, (s - 1) * devices + i) for s in range(1, sections) for i in range(devices)]
    relay_onward = [(s * devices + a, (s - 1) * devices + b) for s in range(1, sections) for a, b in onward]

    me = lax.axis_index("expert")
    origins = lax.dynamic_index_in_dim(jnp.asarray(origin_table(devices, tour)), me, 0, keepdims=False)

    rows = grad_out[0]
    tokens = rows.shape[0]
    hidden = saved_gate.shape[3]
    capacity = saved_gate.shape[2] // devices
    piece = tokens // PIECES
    first = [rows[h * piece:(h + 1) * piece] for h in range(PIECES)]
    first, routing, weights = lax.optimization_barrier((first, expert_ids[0], gate_weights[0]))

    blocks = [first]
    for _ in range(1, chips):
        blocks.append([lax.ppermute(b, "expert", onward) for b in blocks[-1]])
    others = []
    for step in range(chips):
        others.append([lax.ppermute(b, "expert", swap) for b in blocks[step]])

    experts = jnp.arange(devices, dtype=jnp.int32)
    chosen = routing[:, None, :] == experts[None, :, None]
    named = jnp.any(chosen, axis=2)
    weight_of = jnp.sum(jnp.where(chosen, weights[:, None, :], 0.0), axis=2)
    earlier = jnp.tril(jnp.ones((tokens, tokens), jnp.bfloat16), -1)
    position = lax.dot_general(
        earlier, named.astype(jnp.bfloat16), (((1,), (0,)), ((), ())), preferred_element_type=jnp.float32
    )
    position = jnp.where(named, position, -1.0)
    table = jnp.stack([position.T, weight_of.T], axis=1)
    table = lax.all_to_all(table, "expert", split_axis=0, concat_axis=0, tiled=True)

    gate_rows = saved_gate[0, 0].reshape(devices, capacity, hidden)
    up_rows = saved_up[0, 0].reshape(devices, capacity, hidden)

    matrices, others[0], table = lax.optimization_barrier(((w_down[0, 0], w_gate[0, 0], w_up[0, 0]), others[0], table))
    matrices = load_inside(*matrices)
    running = own = None
    token = origins
    for step in range(chips):
        parts = expert_step(
            token[step], blocks[step], others[step], table, gate_rows, up_rows, *matrices
        )
        token, *parts = lax.optimization_barrier((token, *parts))
        given = [lax.ppermute(p, "expert", swap) for p in parts[PIECES:]]
        total = [a + b.astype(jnp.float32) for a, b in zip(parts[:PIECES], given)]
        if step == 0:
            own = [lax.ppermute(c.astype(jnp.bfloat16), ("section", "expert"), relay) for c in total]
        elif step == 1:
            running = [c.astype(jnp.bfloat16) for c in total]
        else:
            arrived = [lax.ppermute(r, "expert", onward) for r in running]
            running = [(a.astype(jnp.float32) + c).astype(jnp.bfloat16) for a, c in zip(arrived, total)]
    last = [lax.ppermute(r, ("section", "expert"), relay_onward) for r in running]
    result = [(a.astype(jnp.float32) + b.astype(jnp.float32)).astype(jnp.bfloat16) for a, b in zip(last, own)]
    return jnp.concatenate(result, axis=0)[None]


def solution(mesh):
    placed = (
        P("section", "expert", None),
        P("section", "expert", None),
        P("section", "expert", None),
        P("section", "expert", None, None),
        P("section", "expert", None, None),
        P("section", "expert", None, None),
        P("section", "expert", None, None),
        P("section", "expert", None, None),
    )
    return jax.shard_map(body, mesh=mesh, in_specs=placed, out_specs=P("section", "expert", None), check_vma=False)
```

```python
import math

import jax
import jax.numpy as jnp
import numpy as np
from jax import lax
from jax.experimental import pallas as pl
from jax.experimental.pallas import tpu as pltpu
from jax.sharding import PartitionSpec as P


PIECES = 2
HIDDEN_BLOCK = 256
PART = 1024
VMEM_LIMIT = 16 << 20
CONTRACT = (((1,), (1,)), ((), ()))


def chip_ring(chips):
    width = 1 << (int(math.log2(chips)) // 2)
    height = chips // width
    tour = []
    for row in range(height):
        columns = list(range(1, width))
        if row % 2:
            columns.reverse()
        tour += [row * width + column for column in columns]
    return tour + [row * width for row in reversed(range(height))]


def origin_table(devices, tour):
    chips = len(tour)
    place = {chip: k for k, chip in enumerate(tour)}
    table = np.zeros((devices, chips, 2), np.int32)
    for device in range(devices):
        at = place[device // 2]
        for step in range(chips):
            by_core = [2 * tour[(at - step) % chips], 2 * tour[(at + step) % chips] + 1]
            table[device, step] = by_core[device % 2], by_core[1 - device % 2]
    return table


def expert_kernel(
    origin, a0, a1, b0, b1, table, saved_gate, saved_up, w_down, w_wide, mine, given,
    block, entry, gate_rows, up_rows, gate_slope, up_slope, joined_grad, scale, out_mine, out_given,
    block_sem, entry_sem, rows_sem, out_sem,
):
    piece, _ = a0.shape
    tokens = 2 * piece
    hidden = w_down.shape[0]
    parts, _, part = out_mine.shape
    capacity = gate_rows.shape[1]

    def block_copy(n):
        return pltpu.make_async_copy((a0, a1, b0, b1)[n], block.at[pl.ds(n * piece, piece)], block_sem.at[n])

    def entry_copy(n):
        return pltpu.make_async_copy(table.at[origin[n]], entry.at[n], entry_sem.at[n])

    def gate_rows_copy(n):
        return pltpu.make_async_copy(saved_gate.at[origin[n]], gate_rows.at[n], rows_sem.at[n])

    def up_rows_copy(n):
        return pltpu.make_async_copy(saved_up.at[origin[n]], up_rows.at[n], rows_sem.at[2 + n])

    for n in range(2):
        entry_copy(n).start()
        gate_rows_copy(n).start()
        up_rows_copy(n).start()
    for n in range(4):
        block_copy(n).start()
    for n in range(2):
        entry_copy(n).wait()
        gate_rows_copy(n).wait()
        up_rows_copy(n).wait()
    for n in range(2):
        rows = pl.ds(n * tokens, tokens)
        place = jnp.broadcast_to(entry[n, 0:1, :], (tokens, tokens)).T
        slot = lax.broadcasted_iota(jnp.int32, (tokens, tokens), 1).astype(jnp.float32)
        pick = jnp.where(place == slot, 1.0, 0.0).astype(jnp.bfloat16)[:, :capacity]
        scale[rows, :] = jnp.broadcast_to(entry[n, 1:2, :], (tokens, tokens)).T
        gate = jnp.dot(pick, gate_rows[n], preferred_element_type=jnp.float32)
        up = jnp.dot(pick, up_rows[n], preferred_element_type=jnp.float32)
        sig = 1.0 / (1.0 + jnp.exp(-gate))
        gate_slope[rows, :] = up * sig * (1.0 + gate * (1.0 - sig))
        up_slope[rows, :] = gate * sig
    for n in range(4):
        block_copy(n).wait()

    for k in range(hidden // HIDDEN_BLOCK):
        columns = pl.ds(k * HIDDEN_BLOCK, HIDDEN_BLOCK)
        hidden_grad = lax.dot_general(block[...], w_down[columns, :], CONTRACT, preferred_element_type=jnp.float32)
        joined_grad[:, columns] = (hidden_grad * gate_slope[:, columns]).astype(jnp.bfloat16)
        up_columns = pl.ds(hidden + k * HIDDEN_BLOCK, HIDDEN_BLOCK)
        joined_grad[:, up_columns] = (hidden_grad * up_slope[:, columns]).astype(jnp.bfloat16)

    outs = (mine, given)

    def out_copy(j, n):
        columns = pl.ds(pl.multiple_of(j * part, part), part)
        return pltpu.make_async_copy((out_mine, out_given)[n].at[j], outs[n].at[:, columns], out_sem.at[j, n])

    def wide_step(j, carry):
        columns = pl.ds(pl.multiple_of(j * part, part), part)
        back = lax.dot_general(joined_grad[...], w_wide[columns, :], CONTRACT, preferred_element_type=jnp.float32)
        weight = jnp.concatenate([scale[...]] * (part // tokens), axis=1)
        back = back.astype(jnp.bfloat16).astype(jnp.float32) * weight
        out_mine[j] = back[:tokens]
        out_given[j] = back[tokens:].astype(jnp.bfloat16)
        for n in range(2):
            out_copy(j, n).start()
        return carry

    lax.fori_loop(0, parts, wide_step, 0)

    def drain(j, carry):
        for n in range(2):
            out_copy(j, n).wait()
        return carry

    lax.fori_loop(0, parts, drain, 0)


def expert_step(origin, held, other, table, gate_rows, up_rows, w_down, w_wide):
    piece, width = held[0].shape
    tokens = 2 * piece
    hidden = w_down.shape[0]
    capacity = gate_rows.shape[1]
    parts = width // PART
    anywhere, inside = pl.BlockSpec(memory_space=pl.ANY), pl.BlockSpec(memory_space=pltpu.VMEM)
    bf16, f32 = jnp.bfloat16, jnp.float32
    dma = pltpu.SemaphoreType.DMA
    flops = 2 * 2 * tokens * hidden * width * 3
    moved = 2 * tokens * width * 10
    weights = [pltpu.with_memory_space_constraint(w, pltpu.VMEM) for w in (w_down, w_wide)]
    return pl.pallas_call(
        expert_kernel,
        in_specs=[pl.BlockSpec(memory_space=pltpu.SMEM)] + [anywhere] * 7 + [inside] * 2,
        out_specs=[anywhere] * 2,
        out_shape=[jax.ShapeDtypeStruct((tokens, width), f32), jax.ShapeDtypeStruct((tokens, width), bf16)],
        scratch_shapes=[
            pltpu.VMEM((2 * tokens, width), bf16),
            pltpu.VMEM((2,) + table.shape[1:], f32),
            pltpu.VMEM((2, capacity, hidden), bf16),
            pltpu.VMEM((2, capacity, hidden), bf16),
            pltpu.VMEM((2 * tokens, hidden), f32),
            pltpu.VMEM((2 * tokens, hidden), f32),
            pltpu.VMEM((2 * tokens, 2 * hidden), bf16),
            pltpu.VMEM((2 * tokens, tokens), f32),
            pltpu.VMEM((parts, tokens, PART), f32),
            pltpu.VMEM((parts, tokens, PART), bf16),
            dma((4,)),
            dma((2,)),
            dma((4,)),
            dma((parts, 2)),
        ],
        compiler_params=pltpu.CompilerParams(vmem_limit_bytes=VMEM_LIMIT),
        cost_estimate=pl.CostEstimate(flops=flops, transcendentals=2 * tokens * hidden, bytes_accessed=moved),
        name="expert_step",
    )(origin, *held, *other, table, gate_rows, up_rows, *weights)


def load_kernel(w_down, w_gate, w_up, down, wide, sem):
    hidden = w_gate.shape[1]
    copies = [
        pltpu.make_async_copy(w_down, down, sem.at[0]),
        pltpu.make_async_copy(w_gate, wide.at[:, pl.ds(0, hidden)], sem.at[1]),
        pltpu.make_async_copy(w_up, wide.at[:, pl.ds(hidden, hidden)], sem.at[2]),
    ]
    for copy in copies:
        copy.start()
    for copy in copies:
        copy.wait()


def load_inside(*arrays):
    w_down, w_gate, w_up = arrays
    return pl.pallas_call(
        load_kernel,
        in_specs=[pl.BlockSpec(memory_space=pltpu.HBM)] * 3,
        out_specs=[pl.BlockSpec(memory_space=pltpu.VMEM)] * 2,
        out_shape=[
            pltpu.VMEM(w_down.shape, w_down.dtype),
            pltpu.VMEM((w_gate.shape[0], w_gate.shape[1] + w_up.shape[1]), w_gate.dtype),
        ],
        scratch_shapes=[pltpu.SemaphoreType.DMA((3,))],
        compiler_params=pltpu.CompilerParams(vmem_limit_bytes=VMEM_LIMIT),
        name="load_weights",
    )(*[pltpu.with_memory_space_constraint(a, pltpu.HBM) for a in arrays])


def body(grad_out, expert_ids, gate_weights, saved_gate, saved_up, w_gate, w_up, w_down):
    devices = lax.axis_size("expert")
    sections = lax.axis_size("section")
    chips = devices // 2
    tour = chip_ring(chips)
    following = {chip: tour[(k + 1) % chips] for k, chip in enumerate(tour)}
    onward = [(2 * a, 2 * b) for a, b in following.items()] + [(2 * b + 1, 2 * a + 1) for a, b in following.items()]
    swap = [(i, i ^ 1) for i in range(devices)]
    relay = [(s * devices + i, (s - 1) * devices + i) for s in range(1, sections) for i in range(devices)]
    relay_onward = [(s * devices + a, (s - 1) * devices + b) for s in range(1, sections) for a, b in onward]

    me = lax.axis_index("expert")
    origins = lax.dynamic_index_in_dim(jnp.asarray(origin_table(devices, tour)), me, 0, keepdims=False)

    rows = grad_out[0]
    tokens = rows.shape[0]
    hidden = saved_gate.shape[3]
    capacity = saved_gate.shape[2] // devices
    piece = tokens // PIECES
    first = [rows[h * piece:(h + 1) * piece] for h in range(PIECES)]
    first, routing, weights = lax.optimization_barrier((first, expert_ids[0], gate_weights[0]))

    blocks = [first]
    for _ in range(1, chips):
        blocks.append([lax.ppermute(b, "expert", onward) for b in blocks[-1]])
    others = []
    for step in range(chips):
        others.append([lax.ppermute(b, "expert", swap) for b in blocks[step]])

    experts = jnp.arange(devices, dtype=jnp.int32)
    chosen = routing[:, None, :] == experts[None, :, None]
    named = jnp.any(chosen, axis=2)
    weight_of = jnp.sum(jnp.where(chosen, weights[:, None, :], 0.0), axis=2)
    earlier = jnp.tril(jnp.ones((tokens, tokens), jnp.bfloat16), -1)
    position = lax.dot_general(
        earlier, named.astype(jnp.bfloat16), (((1,), (0,)), ((), ())), preferred_element_type=jnp.float32
    )
    position = jnp.where(named, position, -1.0)
    table = jnp.stack([position.T, weight_of.T], axis=1)
    table = lax.all_to_all(table, "expert", split_axis=0, concat_axis=0, tiled=True)

    gate_rows = saved_gate[0, 0].reshape(devices, capacity, hidden)
    up_rows = saved_up[0, 0].reshape(devices, capacity, hidden)

    matrices, others[0], table = lax.optimization_barrier(((w_down[0, 0], w_gate[0, 0], w_up[0, 0]), others[0], table))
    matrices = load_inside(*matrices)
    running, own = [], []
    token = origins
    for step in range(chips):
        mine, given = expert_step(
            token[step], blocks[step], others[step], table, gate_rows, up_rows, *matrices
        )
        token, mine, given = lax.optimization_barrier((token, mine, given))
        given = lax.ppermute(given, "expert", swap)
        if step == 1:
            running = [None] * PIECES
        for h in range(PIECES):
            rows = slice(h * piece, (h + 1) * piece)
            total = mine[rows] + given[rows].astype(jnp.float32)
            if step == 0:
                own.append(lax.ppermute(total.astype(jnp.bfloat16), ("section", "expert"), relay))
                kept = own
            else:
                if step > 1:
                    total = lax.ppermute(running[h], "expert", onward).astype(jnp.float32) + total
                running[h] = total.astype(jnp.bfloat16)
                kept = running
            if step > 0 and h + 1 < PIECES:
                kept[h], mine, given = lax.optimization_barrier((kept[h], mine, given))
    last = [lax.ppermute(r, ("section", "expert"), relay_onward) for r in running]
    result = [(a.astype(jnp.float32) + b.astype(jnp.float32)).astype(jnp.bfloat16) for a, b in zip(last, own)]
    return jnp.concatenate(result, axis=0)[None]


def solution(mesh):
    placed = (
        P("section", "expert", None),
        P("section", "expert", None),
        P("section", "expert", None),
        P("section", "expert", None, None),
        P("section", "expert", None, None),
        P("section", "expert", None, None),
        P("section", "expert", None, None),
        P("section", "expert", None, None),
    )
    return jax.shard_map(body, mesh=mesh, in_specs=placed, out_specs=P("section", "expert", None), check_vma=False)
```

```python
import math

import jax
import jax.numpy as jnp
import numpy as np
from jax import lax
from jax.experimental import pallas as pl
from jax.experimental.pallas import tpu as pltpu
from jax.sharding import PartitionSpec as P


PIECES = 2
HIDDEN_BLOCK = 256
PART = 1024
VMEM_LIMIT = 10 << 20
CONTRACT = (((1,), (1,)), ((), ()))


def chip_ring(chips):
    width = 1 << (int(math.log2(chips)) // 2)
    height = chips // width
    tour = []
    for row in range(height):
        columns = list(range(1, width))
        if row % 2:
            columns.reverse()
        tour += [row * width + column for column in columns]
    return tour + [row * width for row in reversed(range(height))]


def origin_table(devices, tour):
    chips = len(tour)
    place = {chip: k for k, chip in enumerate(tour)}
    table = np.zeros((devices, chips, 2), np.int32)
    for device in range(devices):
        at = place[device // 2]
        for step in range(chips):
            by_core = [2 * tour[(at - step) % chips], 2 * tour[(at + step) % chips] + 1]
            table[device, step] = by_core[device % 2], by_core[1 - device % 2]
    return table


def expert_kernel(
    origin, a0, a1, b0, b1, table, saved_gate, saved_up, w_down, w_wide, mine, given,
    block, entry, gate_rows, up_rows, gate_slope, up_slope, joined_grad, scale, out_mine, out_given,
    block_sem, entry_sem, rows_sem, out_sem,
):
    piece, _ = a0.shape
    tokens = 2 * piece
    hidden = w_down.shape[0]
    parts, _, part = out_mine.shape
    capacity = gate_rows.shape[1]

    def block_copy(n):
        return pltpu.make_async_copy((a0, a1, b0, b1)[n], block.at[pl.ds(n * piece, piece)], block_sem.at[n])

    def entry_copy(n):
        return pltpu.make_async_copy(table.at[origin[n]], entry.at[n], entry_sem.at[n])

    def gate_rows_copy(n):
        return pltpu.make_async_copy(saved_gate.at[origin[n]], gate_rows.at[n], rows_sem.at[n])

    def up_rows_copy(n):
        return pltpu.make_async_copy(saved_up.at[origin[n]], up_rows.at[n], rows_sem.at[2 + n])

    for n in range(2):
        entry_copy(n).start()
        gate_rows_copy(n).start()
        up_rows_copy(n).start()
    for n in range(4):
        block_copy(n).start()
    for n in range(2):
        entry_copy(n).wait()
        gate_rows_copy(n).wait()
        up_rows_copy(n).wait()
    for n in range(2):
        rows = pl.ds(n * tokens, tokens)
        place = jnp.broadcast_to(entry[n, 0:1, :], (tokens, tokens)).T
        slot = lax.broadcasted_iota(jnp.int32, (tokens, tokens), 1).astype(jnp.float32)
        pick = jnp.where(place == slot, 1.0, 0.0).astype(jnp.bfloat16)[:, :capacity]
        scale[rows, :] = jnp.broadcast_to(entry[n, 1:2, :], (tokens, tokens)).T
        gate = jnp.dot(pick, gate_rows[n], preferred_element_type=jnp.float32)
        up = jnp.dot(pick, up_rows[n], preferred_element_type=jnp.float32)
        sig = 1.0 / (1.0 + jnp.exp(-gate))
        gate_slope[rows, :] = up * sig * (1.0 + gate * (1.0 - sig))
        up_slope[rows, :] = gate * sig
    for n in range(4):
        block_copy(n).wait()

    for k in range(hidden // HIDDEN_BLOCK):
        columns = pl.ds(k * HIDDEN_BLOCK, HIDDEN_BLOCK)
        hidden_grad = lax.dot_general(block[...], w_down[columns, :], CONTRACT, preferred_element_type=jnp.float32)
        joined_grad[:, columns] = (hidden_grad * gate_slope[:, columns]).astype(jnp.bfloat16)
        up_columns = pl.ds(hidden + k * HIDDEN_BLOCK, HIDDEN_BLOCK)
        joined_grad[:, up_columns] = (hidden_grad * up_slope[:, columns]).astype(jnp.bfloat16)

    outs = (mine, given)

    def out_copy(j, n):
        columns = pl.ds(pl.multiple_of(j * part, part), part)
        return pltpu.make_async_copy((out_mine, out_given)[n].at[j], outs[n].at[:, columns], out_sem.at[j, n])

    def wide_step(j, carry):
        columns = pl.ds(pl.multiple_of(j * part, part), part)
        back = lax.dot_general(joined_grad[...], w_wide[columns, :], CONTRACT, preferred_element_type=jnp.float32)
        weight = jnp.concatenate([scale[...]] * (part // tokens), axis=1)
        back = back.astype(jnp.bfloat16).astype(jnp.float32) * weight
        out_mine[j] = back[:tokens]
        out_given[j] = back[tokens:].astype(jnp.bfloat16)
        for n in range(2):
            out_copy(j, n).start()
        return carry

    lax.fori_loop(0, parts, wide_step, 0)

    def drain(j, carry):
        for n in range(2):
            out_copy(j, n).wait()
        return carry

    lax.fori_loop(0, parts, drain, 0)


def expert_step(origin, held, other, table, gate_rows, up_rows, w_down, w_wide):
    piece, width = held[0].shape
    tokens = 2 * piece
    hidden = w_down.shape[0]
    capacity = gate_rows.shape[1]
    parts = width // PART
    anywhere, inside = pl.BlockSpec(memory_space=pl.ANY), pl.BlockSpec(memory_space=pltpu.VMEM)
    bf16, f32 = jnp.bfloat16, jnp.float32
    dma = pltpu.SemaphoreType.DMA
    flops = 2 * 2 * tokens * hidden * width * 3
    moved = 2 * tokens * width * 10
    weights = [pltpu.with_memory_space_constraint(w, pltpu.VMEM) for w in (w_down, w_wide)]
    return pl.pallas_call(
        expert_kernel,
        in_specs=[pl.BlockSpec(memory_space=pltpu.SMEM)] + [anywhere] * 7 + [inside] * 2,
        out_specs=[anywhere] * 2,
        out_shape=[jax.ShapeDtypeStruct((tokens, width), f32), jax.ShapeDtypeStruct((tokens, width), bf16)],
        scratch_shapes=[
            pltpu.VMEM((2 * tokens, width), bf16),
            pltpu.VMEM((2,) + table.shape[1:], f32),
            pltpu.VMEM((2, capacity, hidden), bf16),
            pltpu.VMEM((2, capacity, hidden), bf16),
            pltpu.VMEM((2 * tokens, hidden), f32),
            pltpu.VMEM((2 * tokens, hidden), f32),
            pltpu.VMEM((2 * tokens, 2 * hidden), bf16),
            pltpu.VMEM((2 * tokens, tokens), f32),
            pltpu.VMEM((parts, tokens, PART), f32),
            pltpu.VMEM((parts, tokens, PART), bf16),
            dma((4,)),
            dma((2,)),
            dma((4,)),
            dma((parts, 2)),
        ],
        compiler_params=pltpu.CompilerParams(vmem_limit_bytes=VMEM_LIMIT),
        cost_estimate=pl.CostEstimate(flops=flops, transcendentals=2 * tokens * hidden, bytes_accessed=moved),
        name="expert_step",
    )(origin, *held, *other, table, gate_rows, up_rows, *weights)


def load_kernel(w_down, w_gate, w_up, down, wide, sem):
    hidden = w_gate.shape[1]
    copies = [
        pltpu.make_async_copy(w_down, down, sem.at[0]),
        pltpu.make_async_copy(w_gate, wide.at[:, pl.ds(0, hidden)], sem.at[1]),
        pltpu.make_async_copy(w_up, wide.at[:, pl.ds(hidden, hidden)], sem.at[2]),
    ]
    for copy in copies:
        copy.start()
    for copy in copies:
        copy.wait()


def load_inside(*arrays):
    w_down, w_gate, w_up = arrays
    return pl.pallas_call(
        load_kernel,
        in_specs=[pl.BlockSpec(memory_space=pltpu.HBM)] * 3,
        out_specs=[pl.BlockSpec(memory_space=pltpu.VMEM)] * 2,
        out_shape=[
            pltpu.VMEM(w_down.shape, w_down.dtype),
            pltpu.VMEM((w_gate.shape[0], w_gate.shape[1] + w_up.shape[1]), w_gate.dtype),
        ],
        scratch_shapes=[pltpu.SemaphoreType.DMA((3,))],
        compiler_params=pltpu.CompilerParams(vmem_limit_bytes=VMEM_LIMIT),
        name="load_weights",
    )(*[pltpu.with_memory_space_constraint(a, pltpu.HBM) for a in arrays])


def widen_kernel(held, out):
    out[...] = held[...].astype(jnp.float32)


def widen(held):
    return pl.pallas_call(
        widen_kernel,
        out_shape=jax.ShapeDtypeStruct(held.shape, jnp.float32),
        compiler_params=pltpu.CompilerParams(vmem_limit_bytes=VMEM_LIMIT),
        name="widen",
    )(held)


def body(grad_out, expert_ids, gate_weights, saved_gate, saved_up, w_gate, w_up, w_down):
    devices = lax.axis_size("expert")
    sections = lax.axis_size("section")
    chips = devices // 2
    tour = chip_ring(chips)
    following = {chip: tour[(k + 1) % chips] for k, chip in enumerate(tour)}
    onward = [(2 * a, 2 * b) for a, b in following.items()] + [(2 * b + 1, 2 * a + 1) for a, b in following.items()]
    swap = [(i, i ^ 1) for i in range(devices)]
    relay = [(s * devices + i, (s - 1) * devices + i) for s in range(1, sections) for i in range(devices)]
    relay_onward = [(s * devices + a, (s - 1) * devices + b) for s in range(1, sections) for a, b in onward]

    me = lax.axis_index("expert")
    origins = lax.dynamic_index_in_dim(jnp.asarray(origin_table(devices, tour)), me, 0, keepdims=False)

    rows = grad_out[0]
    tokens = rows.shape[0]
    hidden = saved_gate.shape[3]
    capacity = saved_gate.shape[2] // devices
    piece = tokens // PIECES
    first = [rows[h * piece:(h + 1) * piece] for h in range(PIECES)]
    first, routing, weights = lax.optimization_barrier((first, expert_ids[0], gate_weights[0]))

    blocks = [first]
    for _ in range(1, chips):
        blocks.append([lax.ppermute(b, "expert", onward) for b in blocks[-1]])
    others = []
    for step in range(chips):
        others.append([lax.ppermute(b, "expert", swap) for b in blocks[step]])

    experts = jnp.arange(devices, dtype=jnp.int32)
    chosen = routing[:, None, :] == experts[None, :, None]
    named = jnp.any(chosen, axis=2)
    weight_of = jnp.sum(jnp.where(chosen, weights[:, None, :], 0.0), axis=2)
    earlier = jnp.tril(jnp.ones((tokens, tokens), jnp.bfloat16), -1)
    position = lax.dot_general(
        earlier, named.astype(jnp.bfloat16), (((1,), (0,)), ((), ())), preferred_element_type=jnp.float32
    )
    position = jnp.where(named, position, -1.0)
    table = jnp.stack([position.T, weight_of.T], axis=1)
    table = lax.all_to_all(table, "expert", split_axis=0, concat_axis=0, tiled=True)

    gate_rows = saved_gate[0, 0].reshape(devices, capacity, hidden)
    up_rows = saved_up[0, 0].reshape(devices, capacity, hidden)

    matrices, others[0], table = lax.optimization_barrier(((w_down[0, 0], w_gate[0, 0], w_up[0, 0]), others[0], table))
    matrices = load_inside(*matrices)
    running, own = [], []
    token = origins
    for step in range(chips):
        mine, given = expert_step(
            token[step], blocks[step], others[step], table, gate_rows, up_rows, *matrices
        )
        token, mine, given = lax.optimization_barrier((token, mine, given))
        given = lax.ppermute(given, "expert", swap)
        if step == 1:
            running = [None] * PIECES
        for h in range(PIECES):
            rows = slice(h * piece, (h + 1) * piece)
            total = mine[rows] + given[rows].astype(jnp.float32)
            if step == 0:
                own.append(lax.ppermute(total.astype(jnp.bfloat16), ("section", "expert"), relay))
                kept = own
            else:
                if step > 1:
                    total = lax.ppermute(running[h], "expert", onward).astype(jnp.float32) + total
                running[h] = total.astype(jnp.bfloat16)
                kept = running
            if step > 0 and h + 1 < PIECES:
                kept[h], mine, given = lax.optimization_barrier((kept[h], mine, given))
    last = []
    for h in range(PIECES):
        last.append(lax.ppermute(running[h], ("section", "expert"), relay_onward))
    own[0] = widen(own[0])
    result = [(a.astype(jnp.float32) + b.astype(jnp.float32)).astype(jnp.bfloat16) for a, b in zip(last, own)]
    return jnp.concatenate(result, axis=0)[None]


def solution(mesh):
    placed = (
        P("section", "expert", None),
        P("section", "expert", None),
        P("section", "expert", None),
        P("section", "expert", None, None),
        P("section", "expert", None, None),
        P("section", "expert", None, None),
        P("section", "expert", None, None),
        P("section", "expert", None, None),
    )
    return jax.shard_map(body, mesh=mesh, in_specs=placed, out_specs=P("section", "expert", None), check_vma=False)
```

```python
import math

import jax
import jax.numpy as jnp
import numpy as np
from jax import lax
from jax.experimental import pallas as pl
from jax.experimental.pallas import tpu as pltpu
from jax.sharding import PartitionSpec as P


PIECES = 2
HIDDEN_BLOCK = 256
PART = 1024
VMEM_LIMIT = 10 << 20
CONTRACT = (((1,), (1,)), ((), ()))


def chip_ring(chips):
    width = 1 << (int(math.log2(chips)) // 2)
    height = chips // width
    tour = []
    for row in range(height):
        columns = list(range(1, width))
        if row % 2:
            columns.reverse()
        tour += [row * width + column for column in columns]
    return tour + [row * width for row in reversed(range(height))]


def origin_table(devices, tour):
    chips = len(tour)
    place = {chip: k for k, chip in enumerate(tour)}
    table = np.zeros((devices, chips, 2), np.int32)
    for device in range(devices):
        at = place[device // 2]
        for step in range(chips):
            by_core = [2 * tour[(at - step) % chips], 2 * tour[(at + step) % chips] + 1]
            table[device, step] = by_core[device % 2], by_core[1 - device % 2]
    return table


def expert_kernel(
    origin, a0, a1, b0, b1, table, saved_gate, saved_up, w_down, w_wide, mine, given,
    block, entry, gate_rows, up_rows, gate_slope, up_slope, joined_grad, scale, out_mine, out_given,
    block_sem, entry_sem, rows_sem, out_sem,
):
    piece, _ = a0.shape
    tokens = 2 * piece
    hidden = w_down.shape[0]
    parts, _, part = out_mine.shape
    capacity = gate_rows.shape[1]

    def block_copy(n):
        return pltpu.make_async_copy((a0, a1, b0, b1)[n], block.at[pl.ds(n * piece, piece)], block_sem.at[n])

    def entry_copy(n):
        return pltpu.make_async_copy(table.at[origin[n]], entry.at[n], entry_sem.at[n])

    def gate_rows_copy(n):
        return pltpu.make_async_copy(saved_gate.at[origin[n]], gate_rows.at[n], rows_sem.at[n])

    def up_rows_copy(n):
        return pltpu.make_async_copy(saved_up.at[origin[n]], up_rows.at[n], rows_sem.at[2 + n])

    for n in range(2):
        entry_copy(n).start()
        gate_rows_copy(n).start()
        up_rows_copy(n).start()
    for n in range(4):
        block_copy(n).start()
    for n in range(2):
        entry_copy(n).wait()
        gate_rows_copy(n).wait()
        up_rows_copy(n).wait()
    picks = []
    for n in range(2):
        rows = pl.ds(n * tokens, tokens)
        place = jnp.broadcast_to(entry[n, 0:1, :], (tokens, tokens)).T
        slot = lax.broadcasted_iota(jnp.int32, (tokens, tokens), 1).astype(jnp.float32)
        pick = jnp.where(place == slot, 1.0, 0.0).astype(jnp.bfloat16)[:, :capacity]
        scale[rows, :] = jnp.broadcast_to(entry[n, 1:2, :], (tokens, tokens)).T
        picks.append(pick)
    for n in range(4):
        block_copy(n).wait()

    for k in range(hidden // HIDDEN_BLOCK):
        columns = pl.ds(k * HIDDEN_BLOCK, HIDDEN_BLOCK)
        hidden_grad = lax.dot_general(block[...], w_down[columns, :], CONTRACT, preferred_element_type=jnp.float32)
        up_columns = pl.ds(hidden + k * HIDDEN_BLOCK, HIDDEN_BLOCK)
        for n in range(2):
            rows = pl.ds(n * tokens, tokens)
            gate = jnp.dot(picks[n], gate_rows[n, :, columns], preferred_element_type=jnp.float32)
            up = jnp.dot(picks[n], up_rows[n, :, columns], preferred_element_type=jnp.float32)
            sig = 1.0 / (1.0 + jnp.exp(-gate))
            grad = hidden_grad[n * tokens:(n + 1) * tokens]
            joined_grad[rows, columns] = (grad * (up * sig * (1.0 + gate * (1.0 - sig)))).astype(jnp.bfloat16)
            joined_grad[rows, up_columns] = (grad * (gate * sig)).astype(jnp.bfloat16)

    outs = (mine, given)

    def out_copy(j, n):
        columns = pl.ds(pl.multiple_of(j * part, part), part)
        return pltpu.make_async_copy((out_mine, out_given)[n].at[j], outs[n].at[:, columns], out_sem.at[j, n])

    def wide_step(j, carry):
        columns = pl.ds(pl.multiple_of(j * part, part), part)
        back = lax.dot_general(joined_grad[...], w_wide[columns, :], CONTRACT, preferred_element_type=jnp.float32)
        weight = jnp.concatenate([scale[...]] * (part // tokens), axis=1)
        back = back.astype(jnp.bfloat16).astype(jnp.float32) * weight
        out_mine[j] = back[:tokens]
        out_given[j] = back[tokens:].astype(jnp.bfloat16)
        for n in range(2):
            out_copy(j, n).start()
        return carry

    lax.fori_loop(0, parts, wide_step, 0)

    def drain(j, carry):
        for n in range(2):
            out_copy(j, n).wait()
        return carry

    lax.fori_loop(0, parts, drain, 0)


def expert_step(origin, held, other, table, gate_rows, up_rows, w_down, w_wide):
    piece, width = held[0].shape
    tokens = 2 * piece
    hidden = w_down.shape[0]
    capacity = gate_rows.shape[1]
    parts = width // PART
    anywhere, inside = pl.BlockSpec(memory_space=pl.ANY), pl.BlockSpec(memory_space=pltpu.VMEM)
    bf16, f32 = jnp.bfloat16, jnp.float32
    dma = pltpu.SemaphoreType.DMA
    flops = 2 * 2 * tokens * hidden * width * 3
    moved = 2 * tokens * width * 10
    weights = [pltpu.with_memory_space_constraint(w, pltpu.VMEM) for w in (w_down, w_wide)]
    return pl.pallas_call(
        expert_kernel,
        in_specs=[pl.BlockSpec(memory_space=pltpu.SMEM)] + [anywhere] * 7 + [inside] * 2,
        out_specs=[anywhere] * 2,
        out_shape=[jax.ShapeDtypeStruct((tokens, width), f32), jax.ShapeDtypeStruct((tokens, width), bf16)],
        scratch_shapes=[
            pltpu.VMEM((2 * tokens, width), bf16),
            pltpu.VMEM((2,) + table.shape[1:], f32),
            pltpu.VMEM((2, capacity, hidden), bf16),
            pltpu.VMEM((2, capacity, hidden), bf16),
            pltpu.VMEM((2 * tokens, hidden), f32),
            pltpu.VMEM((2 * tokens, hidden), f32),
            pltpu.VMEM((2 * tokens, 2 * hidden), bf16),
            pltpu.VMEM((2 * tokens, tokens), f32),
            pltpu.VMEM((parts, tokens, PART), f32),
            pltpu.VMEM((parts, tokens, PART), bf16),
            dma((4,)),
            dma((2,)),
            dma((4,)),
            dma((parts, 2)),
        ],
        compiler_params=pltpu.CompilerParams(vmem_limit_bytes=VMEM_LIMIT),
        cost_estimate=pl.CostEstimate(flops=flops, transcendentals=2 * tokens * hidden, bytes_accessed=moved),
        name="expert_step",
    )(origin, *held, *other, table, gate_rows, up_rows, *weights)


def load_kernel(w_down, w_gate, w_up, down, wide, sem):
    hidden = w_gate.shape[1]
    copies = [
        pltpu.make_async_copy(w_down, down, sem.at[0]),
        pltpu.make_async_copy(w_gate, wide.at[:, pl.ds(0, hidden)], sem.at[1]),
        pltpu.make_async_copy(w_up, wide.at[:, pl.ds(hidden, hidden)], sem.at[2]),
    ]
    for copy in copies:
        copy.start()
    for copy in copies:
        copy.wait()


def load_inside(*arrays):
    w_down, w_gate, w_up = arrays
    return pl.pallas_call(
        load_kernel,
        in_specs=[pl.BlockSpec(memory_space=pltpu.HBM)] * 3,
        out_specs=[pl.BlockSpec(memory_space=pltpu.VMEM)] * 2,
        out_shape=[
            pltpu.VMEM(w_down.shape, w_down.dtype),
            pltpu.VMEM((w_gate.shape[0], w_gate.shape[1] + w_up.shape[1]), w_gate.dtype),
        ],
        scratch_shapes=[pltpu.SemaphoreType.DMA((3,))],
        compiler_params=pltpu.CompilerParams(vmem_limit_bytes=VMEM_LIMIT),
        name="load_weights",
    )(*[pltpu.with_memory_space_constraint(a, pltpu.HBM) for a in arrays])


def widen_kernel(held, out):
    out[...] = held[...].astype(jnp.float32)


def widen(held):
    return pl.pallas_call(
        widen_kernel,
        out_shape=jax.ShapeDtypeStruct(held.shape, jnp.float32),
        compiler_params=pltpu.CompilerParams(vmem_limit_bytes=VMEM_LIMIT),
        name="widen",
    )(held)


def body(grad_out, expert_ids, gate_weights, saved_gate, saved_up, w_gate, w_up, w_down):
    devices = lax.axis_size("expert")
    sections = lax.axis_size("section")
    chips = devices // 2
    tour = chip_ring(chips)
    following = {chip: tour[(k + 1) % chips] for k, chip in enumerate(tour)}
    onward = [(2 * a, 2 * b) for a, b in following.items()] + [(2 * b + 1, 2 * a + 1) for a, b in following.items()]
    swap = [(i, i ^ 1) for i in range(devices)]
    relay = [(s * devices + i, (s - 1) * devices + i) for s in range(1, sections) for i in range(devices)]
    relay_onward = [(s * devices + a, (s - 1) * devices + b) for s in range(1, sections) for a, b in onward]

    me = lax.axis_index("expert")
    origins = lax.dynamic_index_in_dim(jnp.asarray(origin_table(devices, tour)), me, 0, keepdims=False)

    rows = grad_out[0]
    tokens = rows.shape[0]
    hidden = saved_gate.shape[3]
    capacity = saved_gate.shape[2] // devices
    piece = tokens // PIECES
    first = [rows[h * piece:(h + 1) * piece] for h in range(PIECES)]
    first, routing, weights = lax.optimization_barrier((first, expert_ids[0], gate_weights[0]))

    blocks = [first]
    for _ in range(1, chips):
        blocks.append([lax.ppermute(b, "expert", onward) for b in blocks[-1]])
    others = []
    for step in range(chips):
        others.append([lax.ppermute(b, "expert", swap) for b in blocks[step]])

    experts = jnp.arange(devices, dtype=jnp.int32)
    chosen = routing[:, None, :] == experts[None, :, None]
    named = jnp.any(chosen, axis=2)
    weight_of = jnp.sum(jnp.where(chosen, weights[:, None, :], 0.0), axis=2)
    earlier = jnp.tril(jnp.ones((tokens, tokens), jnp.bfloat16), -1)
    position = lax.dot_general(
        earlier, named.astype(jnp.bfloat16), (((1,), (0,)), ((), ())), preferred_element_type=jnp.float32
    )
    position = jnp.where(named, position, -1.0)
    table = jnp.stack([position.T, weight_of.T], axis=1)
    table = lax.all_to_all(table, "expert", split_axis=0, concat_axis=0, tiled=True)

    gate_rows = saved_gate[0, 0].reshape(devices, capacity, hidden)
    up_rows = saved_up[0, 0].reshape(devices, capacity, hidden)

    matrices, others[0], table = lax.optimization_barrier(((w_down[0, 0], w_gate[0, 0], w_up[0, 0]), others[0], table))
    matrices = load_inside(*matrices)
    running, own = [], []
    token = origins
    for step in range(chips):
        mine, given = expert_step(
            token[step], blocks[step], others[step], table, gate_rows, up_rows, *matrices
        )
        token, mine, given = lax.optimization_barrier((token, mine, given))
        given = lax.ppermute(given, "expert", swap)
        if step == 1:
            running = [None] * PIECES
        for h in range(PIECES):
            rows = slice(h * piece, (h + 1) * piece)
            total = mine[rows] + given[rows].astype(jnp.float32)
            if step == 0:
                own.append(lax.ppermute(total.astype(jnp.bfloat16), ("section", "expert"), relay))
                kept = own
            else:
                if step > 1:
                    total = lax.ppermute(running[h], "expert", onward).astype(jnp.float32) + total
                running[h] = total.astype(jnp.bfloat16)
                kept = running
            if step > 0 and h + 1 < PIECES:
                kept[h], mine, given = lax.optimization_barrier((kept[h], mine, given))
    last = []
    for h in range(PIECES):
        last.append(lax.ppermute(running[h], ("section", "expert"), relay_onward))
    own[0] = widen(own[0])
    result = [(a.astype(jnp.float32) + b.astype(jnp.float32)).astype(jnp.bfloat16) for a, b in zip(last, own)]
    return jnp.concatenate(result, axis=0)[None]


def solution(mesh):
    placed = (
        P("section", "expert", None),
        P("section", "expert", None),
        P("section", "expert", None),
        P("section", "expert", None, None),
        P("section", "expert", None, None),
        P("section", "expert", None, None),
        P("section", "expert", None, None),
        P("section", "expert", None, None),
    )
    return jax.shard_map(body, mesh=mesh, in_specs=placed, out_specs=P("section", "expert", None), check_vma=False)
```
